32 devices in a mesh: dp: 2 (over x), section: 4 (over y, core), tensor: 4 (over z).
Axes of the slice: x: 2, y: 2, z: 4, core: 2. Of those that a mesh axis runs over, the one named last changes fastest.
Arguments:
- block_in: bfloat16 [64, 2, 4096], P('dp', None, 'tensor'), may hold values from -128 to 128
- weights: bfloat16 [12, 2, 4096, 8192], P('section', None, 'tensor', 'dp'), may hold values from -0.0625 to 0.0625
- gains: float32 [12, 2, 4096], P('section', None, 'tensor'), may hold values from 0.1 to 1.9
- layer_counts: int32 [4], replicated, may hold values from 1 to 3, 8 in all
Outputs:
- block_out: bfloat16 [64, 2, 4096], P('dp', None, 'tensor')
- gram_in: float32 [2, 4096, 2, 4096], P(None, 'tensor', 'dp', 'section')
- gram_cross: float32 [2, 4096, 2, 4096], P(None, 'tensor', 'dp', 'section')
The draws below stay inside these ranges and needn't reach their ends.
Inputs may be any that keep to these rules, and one draw needn't show every extreme that they name: `layer_counts`: each entry is 1 to 3, they sum to 8, and the largest is exactly 3.
All inputs are finite; a program needn't handle non-finite values.
Results may differ from the reference program's by a relative error of at most 0.0093.
Values may be sent and summed in bfloat16 or wider, within the bound.
A program may use at most 192 MiB of HBM per device.

```python
import math
import jax
import jax.numpy as jnp
import numpy as np
from jax import lax

D = 8192
SLOTS = 3
LAYERS = 8
TOKENS = 64
NBLK = 2
BLKW = 4096
QUART = 1024
N_SECTION = 4


def draw_block_in(key, part):
    first, second = jax.random.split(jax.random.fold_in(key, 11), 2)
    position = jnp.arange(BLKW) // QUART
    ramp_up = 3.0 ** (position.astype(jnp.float32) / max(BLKW // QUART - 1, 1))
    ramp_up = ramp_up.reshape(1, 1, BLKW)
    jitter = jnp.exp(jax.random.uniform(second, (1, NBLK, BLKW), minval=0.0, maxval=math.log(2.0)))
    values = jnp.clip(jax.random.normal(first, (TOKENS, NBLK, BLKW)), -4.0, 4.0) * ramp_up * jitter
    return values.astype(jnp.float32).astype(jnp.bfloat16)


def steps_of(rng, extent, pieces, least, largest):
    factor_of, own = 1.0, jax.random.fold_in(rng, 6)
    for axis_at, blocks in pieces:
        draws = jnp.exp(jax.random.uniform(jax.random.fold_in(own, axis_at), (blocks,), jnp.float32, least / len(pieces), largest / len(pieces)))
        factor_of = factor_of * jnp.repeat(draws, extent[axis_at] // blocks).reshape([-1 if axis == axis_at else 1 for axis in range(len(extent))])
    return factor_of


def profile(count, total, limit, lean):
    portions = [(1 << 20) // math.isqrt(standing ** lean) + 1 for standing in range(2, count + 1)]
    surplus, holding = total - limit - (count - 1), [1] * (count - 1)
    while surplus > 0:
        candidates = [i for i in range(count - 1) if holding[i] < limit]
        whole, budget = sum([portions[i] for i in candidates]), surplus
        for i in candidates:
            more = min(limit - holding[i], max(1, budget * portions[i] // whole), surplus)
            holding[i] = holding[i] + more
            surplus = surplus - more
    return np.array([limit] + holding)


def ragged_sizes(rng, count, total, reach, slope):
    if count == 2:
        one = jax.random.randint(rng, (), max(1, total - reach), min(reach, total - 1) + 1)
        return jnp.stack([one, total - one])
    tallies = jnp.asarray(profile(count, total, reach, slope), jnp.int32)
    couples = (count - 1) // 2
    source_of, sink = tallies[1:1 + 2 * couples:2], tallies[2:2 + 2 * couples:2]
    room = jnp.minimum(source_of - 1, reach - sink)
    passed = jax.random.randint(jax.random.fold_in(rng, 1), (couples,), 0, 1 << 20) % (room + 1)
    tallies = tallies.at[1:1 + 2 * couples:2].set(source_of - passed).at[2:2 + 2 * couples:2].set(sink + passed)
    return tallies[jax.random.permutation(jax.random.fold_in(rng, 2), count)]


def gaussian(stream_key, shape, deviation, reach, cuts=(), kind=jnp.bfloat16):
    gain = steps_of(stream_key, shape, cuts, -0.22, 0.18) if cuts else 1.0
    array = jax.random.normal(stream_key, shape, jnp.float32) * deviation * gain
    return jnp.minimum(jnp.maximum(array, -reach), reach).astype(kind)


def setup_inputs(seed: int = 0) -> dict:
    keys = jax.random.split(jax.random.key(seed), 5)
    return {
        "block_in": draw_block_in(jax.random.fold_in(keys[4], 71), 0),
        "weights": gaussian(keys[1], (N_SECTION * SLOTS, NBLK, BLKW, D), D ** -0.5, 0.0625, ((0, 4), (2, 4), (3, 2))),
        "gains": jnp.clip(1.0 + 0.18 * jax.random.normal(keys[2], (N_SECTION * SLOTS, NBLK, BLKW), jnp.float32), 0.1, 1.9),
        "layer_counts": ragged_sizes(keys[3], N_SECTION, LAYERS, SLOTS, 0).astype(jnp.int32),
    }


EPSILON = 1e-05

def run_layer(hidden, matrix, gain_row):
    wide_rows = hidden.astype(jnp.float32)
    mean_square = lax.optimization_barrier(jnp.sum(wide_rows * wide_rows, axis=1, keepdims=True)) / D
    normed = (wide_rows * lax.rsqrt(mean_square + EPSILON) * gain_row[None, :]).astype(jnp.bfloat16)
    update = jnp.dot(normed, matrix, preferred_element_type=jnp.float32).astype(jnp.bfloat16)
    update = lax.optimization_barrier(update)
    return (wide_rows + update.astype(jnp.float32)).astype(jnp.bfloat16)

def reference(block_in, weights, gains, layer_counts):
    block_rows = block_in.reshape(TOKENS, D)
    hidden = block_rows
    for segment_pos in range(N_SECTION):
        for slot_id in range(SLOTS):
            slot_flat = segment_pos * SLOTS + slot_id
            matrix = weights[slot_flat].reshape(D, D)
            gain_row = gains[slot_flat].reshape(D)
            hidden = lax.cond(slot_id < layer_counts[segment_pos], lambda value, mat=matrix, gvec=gain_row: run_layer(value, mat, gvec), lambda value: value, hidden)
    gram_in = jnp.dot(block_rows.T, block_rows, preferred_element_type=jnp.float32) / TOKENS
    gram_cross = jnp.dot(block_rows.T, hidden, preferred_element_type=jnp.float32) / TOKENS
    return (hidden.reshape(TOKENS, NBLK, BLKW), gram_in.reshape(NBLK, BLKW, NBLK, BLKW), gram_cross.reshape(NBLK, BLKW, NBLK, BLKW))
```

```python
import functools

import jax
import jax.numpy as jnp
from jax import lax
from jax.experimental import pallas as pl
from jax.experimental.pallas import tpu as pltpu
from jax.sharding import PartitionSpec as P

LAYERS = 8
EPSILON = 1e-05
MESH = pl.DeviceIdType.MESH
VMEM_LIMIT = 67043328


def windows(ns, slots):
    first = [max(s, LAYERS - slots * (ns - s)) for s in range(ns)]
    last = [min(slots * s, LAYERS - (ns - s)) for s in range(ns)] + [LAYERS]
    return first, last[:ns], last[1:]


def pick(index, values):
    out = jnp.int32(values[0])
    for i in range(1, len(values)):
        out = jnp.where(index == i, jnp.int32(values[i]), out)
    return out


def among(index, members):
    out = index == members[0]
    for m in members[1:]:
        out = out | (index == m)
    return out


def relay(
    nd, ns, nt, slots,
    counts, bi, gains, w_hbm,
    rows_out, cin_out, cout_out, bo_out,
    wv, x0r, xr, hr, hst, xs, xg, ps, pr, own, sss, ssr, cin, fin, cout, bo,
    w_sem, x0_ss, x0_rs, ci_ss, ci_rs, ps_ss, pr_rs, ss_ss, ss_rs, xs_ss, xr_rs, h_ss, h_rs,
    co_ss, co_rs, bo_ss, bo_rs,
):
    nb, tl, q = bi.shape
    T = tl * nd
    tn = min(256, q)
    d, s, t = lax.axis_index("dp"), lax.axis_index("section"), lax.axis_index("tensor")
    first, last, end = windows(ns, slots)

    def tq_of(r):
        return lax.rem(t + r, nt)

    def dp_of(k):
        return lax.rem(d + k, nd)

    def wcopy(k, r):
        cols = pl.ds(pl.multiple_of(tq_of(r) * q, q), q)
        return pltpu.make_async_copy(w_hbm.at[k, :, cols], wv.at[k, :, cols], w_sem.at[k, r - 1])

    def rcopy(src, dst, ss, rs, **to):
        return pltpu.make_async_remote_copy(
            src_ref=src, dst_ref=dst, send_sem=ss, recv_sem=rs,
            device_id={"dp": d, "section": s, "tensor": t, **to}, device_id_type=MESH,
        )

    for k in range(slots):
        for r in range(1, nt + 1):
            wcopy(k, r).start()

    total = nd * ns * nt
    me = (d * ns + s) * nt + t
    barrier = pltpu.get_barrier_semaphore()

    def greet(k, carry):
        o = lax.rem(me + k, total)
        pl.semaphore_signal(
            barrier, inc=1,
            device_id={
                "dp": lax.div(o, ns * nt),
                "section": lax.rem(lax.div(o, nt), ns),
                "tensor": lax.rem(o, nt),
            },
            device_id_type=MESH,
        )
        return carry

    lax.fori_loop(1, total, greet, 0)
    pl.semaphore_wait(barrier, total - 1)

    mine = pl.ds(pl.multiple_of(d * tl, tl), tl)

    def x0copy(k):
        return rcopy(bi, x0r.at[:, mine, :], x0_ss.at[k - 1], x0_rs.at[k - 1], dp=dp_of(k))

    for k in range(1, nd):
        x0copy(k).start()
    x0r[:, mine, :] = bi[...]

    def cicopy(kt, kd):
        to = dp_of(kd)
        return rcopy(
            bi.at[to], cin.at[mine, :], ci_ss, ci_rs.at[kd], dp=to, tensor=tq_of(kt)
        )

    pairs = [(kt, kd) for kt in range(nt) for kd in range(nd) if kt or kd]

    @pl.when(t == s)
    def _():
        for kt, kd in pairs:
            cicopy(kt, kd).start()
        cin[mine, :] = bi[d]

    for k in range(1, nd):
        x0copy(k).wait()

    start = jnp.int32(0)
    for i in range(ns - 1):
        start = start + jnp.where(s > i, counts[i], 0)
    first_s = pick(s, first)
    waited = {i: set() for i in range(ns)}

    def need(j, act):
        spans = {
            i: (max(0, j - last[i]), min(slots - 1, j - first[i])) for i in act
        }
        if all(lo == hi for lo, hi in spans.values()):
            return pick(s, [spans[i][0] if i in spans else 0 for i in range(ns)]), {
                i: {spans[i][0]} for i in act
            }
        return jnp.clip(j - start, 0, slots - 1), {i: set(range(slots)) for i in act}

    def layer(j):
        act = [i for i in range(ns) if first[i] <= j < end[i]]
        par, nxt = j % 2, (j + 1) % 2
        slot, wants = need(j, act)
        takers = [i for i in act if i >= 1 and first[i] <= j <= last[i]]
        fresh = {}
        for i in act:
            fresh[i] = sorted(wants[i] - waited[i])
            waited[i] |= wants[i]

        @pl.when(among(s, act))
        def _():
            hand_id = jnp.clip(j - first_s, 0, hr.shape[0] - 1)
            if takers:
                @pl.when(among(s, takers))
                def _():
                    for kd in range(nd):
                        rcopy(
                            hst.at[0], hr.at[hand_id, 0], h_ss.at[0, kd], h_rs.at[hand_id, kd]
                        ).wait_recv()
                take = among(s, takers) & ((start == j) | (first_s == j))
            gain = gains[slot]
            squares = jnp.zeros((T, 1), jnp.float32)
            for b in range(nb):
                if j == 0:
                    v = x0r[b].astype(jnp.float32)
                elif takers:
                    v = jnp.where(
                        take, hr[hand_id, b].astype(jnp.float32), xr[par, b].astype(jnp.float32)
                    )
                else:
                    v = xr[par, b].astype(jnp.float32)
                xs[b] = v.astype(jnp.bfloat16)
                xg[:, b * q:(b + 1) * q] = (v * gain[:, b * q:(b + 1) * q]).astype(jnp.bfloat16)
                squares = squares + jnp.sum(v * v, axis=1, keepdims=True)
            sss[...] = jnp.broadcast_to(squares, sss.shape)

            def sscopy(r):
                return rcopy(
                    sss, ssr.at[par, r - 1], ss_ss.at[r - 1], ss_rs.at[par, r - 1], tensor=tq_of(r)
                )

            def pscopy(r):
                return rcopy(
                    ps.at[r - 1], pr.at[par, r - 1], ps_ss.at[r - 1], pr_rs.at[par, r - 1],
                    tensor=tq_of(r),
                )

            for r in range(1, nt):
                sscopy(r).start()
            for r in range(1, nt + 1):
                for i in act:
                    if fresh[i]:
                        @pl.when(s == i)
                        def _(i=i):
                            for k in fresh[i]:
                                if r == 1 and len(fresh[i]) > 1:
                                    for rr in range(1, nt + 1):
                                        wcopy(k, rr).wait()
                                elif len(fresh[i]) == 1 and len(wants[i]) == 1:
                                    wcopy(k, r).wait()
                                elif r == 1:
                                    for rr in range(1, nt + 1):
                                        wcopy(k, rr).wait()
                base = tq_of(r) * q

                def tile(i, carry):
                    cols = pl.ds(pl.multiple_of(base + i * tn, tn), tn)
                    acc = jnp.dot(
                        xg[...], wv[slot, :, cols], preferred_element_type=jnp.float32
                    )
                    here = pl.ds(pl.multiple_of(i * tn, tn), tn)
                    if r < nt:
                        ps[r - 1, :, here] = acc.astype(jnp.bfloat16)
                    else:
                        own[:, here] = acc
                    return carry

                lax.fori_loop(0, q // tn, tile, 0)
                if r < nt:
                    pscopy(r).start()
            for r in range(1, nt):
                sscopy(r).wait()
                squares = squares + ssr[par, r - 1][:, :1]
            scale = lax.rsqrt(squares / (nb * q * nt) + EPSILON)
            for r in range(1, nt):
                pscopy(r).wait()
            summed = own[...]
            for r in range(1, nt):
                summed = summed + pr[par, r - 1].astype(jnp.float32)
            update = (summed * scale).astype(jnp.bfloat16)
            new = (xs[d].astype(jnp.float32) + update.astype(jnp.float32)).astype(jnp.bfloat16)
            if j + 1 == LAYERS:
                fin[...] = new
                return
            givers = [i for i in act if i + 1 < ns and first[i + 1] <= j + 1 <= last[i + 1]]
            stay = [i for i in act if j + 1 < end[i]]

            def xcopy(k):
                return rcopy(
                    xr.at[nxt, d], xr.at[nxt, d], xs_ss.at[k - 1], xr_rs.at[nxt, k - 1], dp=dp_of(k)
                )

            if stay:
                @pl.when(among(s, stay))
                def _():
                    xr[nxt, d] = new
                    for k in range(1, nd):
                        xcopy(k).start()
            if givers:
                @pl.when(among(s, givers))
                def _():
                    give_id = pick(s, [j + 1 - first[i + 1] if i in givers else 0 for i in range(ns)])
                    hst[give_id] = new
                    for k in range(nd):
                        rcopy(
                            hst.at[give_id], hr.at[give_id, d], h_ss.at[give_id, k],
                            h_rs.at[give_id, k], dp=dp_of(k), section=s + 1,
                        ).start()
            if stay:
                @pl.when(among(s, stay))
                def _():
                    for k in range(1, nd):
                        xcopy(k).wait()

    for j in range(LAYERS):
        layer(j)

    top = ns - 1

    def cocopy(kt):
        return rcopy(fin, cout, co_ss.at[kt], co_rs, section=t, tensor=tq_of(kt))

    def bocopy(sec, kd):
        to = dp_of(kd)
        part = pl.ds(pl.multiple_of(to * tl, tl), tl)
        return rcopy(
            fin.at[part, :], bo.at[d], bo_ss.at[sec, kd], bo_rs.at[kd], dp=to, section=sec
        )

    outs = [(sec, kd) for sec in range(ns) for kd in range(nd) if sec != top or kd]

    @pl.when(s == top)
    def _():
        for kt in range(1, nt):
            cocopy(kt).start()

        @pl.when(t != top)
        def _():
            cocopy(0).start()

        @pl.when(t == top)
        def _():
            cout[...] = fin[...]

        for sec, kd in outs:
            bocopy(sec, kd).start()
        bo[d] = fin[mine, :]

    for i in range(ns):
        @pl.when(s == i)
        def _(i=i):
            for k in range(slots):
                if k not in waited[i]:
                    for r in range(1, nt + 1):
                        wcopy(k, r).wait()
            if i + 1 < ns:
                for h in range(last[i + 1] - first[i + 1] + 1):
                    for kd in range(nd):
                        rcopy(
                            hst.at[h], hr.at[h, d], h_ss.at[h, kd], h_rs.at[h, kd]
                        ).wait_send()

    @pl.when(t == s)
    def _():
        for kt, kd in pairs:
            cicopy(kt, kd).wait_send()
        for kd in range(1, nd):
            cicopy(1, kd).wait_recv()

    @pl.when(t != s)
    def _():
        for kd in range(nd):
            cicopy(1, kd).wait_recv()

    for b in range(nb):
        rows_out[:, b * q:(b + 1) * q] = x0r[b]
    cin_out[...] = cin[...]

    @pl.when((s != top) | (t != top))
    def _():
        cocopy(1).wait_recv()

    cout_out[...] = cout[...]

    @pl.when(s != top)
    def _():
        for kd in range(nd):
            bocopy(0, kd).wait_recv()

    @pl.when(s == top)
    def _():
        for kd in range(1, nd):
            bocopy(0, kd).wait_recv()
        for kt in range(1, nt):
            cocopy(kt).wait_send()

        @pl.when(t != top)
        def _():
            cocopy(0).wait_send()

        for sec, kd in outs:
            bocopy(sec, kd).wait_send()

    bo_out[...] = bo[...]


def local(nd, ns, nt, block_in, weights, gains, layer_counts):
    tl, nb, q = block_in.shape
    slots, _, _, width = weights.shape
    assert nb == nd and width == nt * q and ns == nt
    T, K = tl * nd, nb * q
    first, last, _ = windows(ns, slots)
    hands = max(last[i] - first[i] + 1 for i in range(1, ns))
    bf, f32 = jnp.bfloat16, jnp.float32
    DMA = pltpu.SemaphoreType.DMA
    vm = pl.BlockSpec(memory_space=pltpu.VMEM)
    rows, cols_in, cols_out, out = pl.pallas_call(
        functools.partial(relay, nd, ns, nt, slots),
        out_shape=(
            jax.ShapeDtypeStruct((T, K), bf),
            jax.ShapeDtypeStruct((T, q), bf),
            jax.ShapeDtypeStruct((T, q), bf),
            jax.ShapeDtypeStruct((nb, tl, q), bf),
        ),
        in_specs=[
            pl.BlockSpec(memory_space=pltpu.SMEM), vm, vm, pl.BlockSpec(memory_space=pl.ANY),
        ],
        out_specs=(vm, vm, vm, vm),
        scratch_shapes=[
            pltpu.VMEM((slots, K, width), bf),
            pltpu.VMEM((nb, T, q), bf),
            pltpu.VMEM((2, nb, T, q), bf),
            pltpu.VMEM((hands, nb, T, q), bf),
            pltpu.VMEM((hands, T, q), bf),
            pltpu.VMEM((nb, T, q), bf),
            pltpu.VMEM((T, K), bf),
            pltpu.VMEM((nt - 1, T, q), bf),
            pltpu.VMEM((2, nt - 1, T, q), bf),
            pltpu.VMEM((T, q), f32),
            pltpu.VMEM((T, 128), f32),
            pltpu.VMEM((2, nt - 1, T, 128), f32),
            pltpu.VMEM((T, q), bf),
            pltpu.VMEM((T, q), bf),
            pltpu.VMEM((T, q), bf),
            pltpu.VMEM((nb, tl, q), bf),
            DMA((slots, nt)), DMA((max(nd - 1, 1),)), DMA((max(nd - 1, 1),)), DMA, DMA((nd,)),
            DMA((nt - 1,)), DMA((2, nt - 1)), DMA((nt - 1,)), DMA((2, nt - 1)),
            DMA((max(nd - 1, 1),)), DMA((2, max(nd - 1, 1))), DMA((hands, nd)), DMA((hands, nd)),
            DMA((nt,)), DMA, DMA((ns, nd)), DMA((nd,)),
        ],
        compiler_params=pltpu.CompilerParams(
            collective_id=0, has_side_effects=True, vmem_limit_bytes=VMEM_LIMIT
        ),
    )(
        layer_counts, block_in.transpose(1, 0, 2), gains.reshape(slots, 1, K),
        weights.reshape(slots, K, width),
    )
    contract = (((0,), (0,)), ((), ()))
    gram_in = lax.dot_general(rows, cols_in, contract, preferred_element_type=f32) / T
    gram_cross = lax.dot_general(rows, cols_out, contract, preferred_element_type=f32) / T
    return (
        out.transpose(1, 0, 2),
        gram_in.reshape(nb, q, 1, q),
        gram_cross.reshape(nb, q, 1, q),
    )


def solution(mesh):
    nd, ns, nt = mesh.shape["dp"], mesh.shape["section"], mesh.shape["tensor"]
    return jax.shard_map(
        functools.partial(local, nd, ns, nt),
        mesh=mesh,
        in_specs=(
            P("dp", None, "tensor"),
            P("section", None, "tensor", "dp"),
            P("section", None, "tensor"),
            P(),
        ),
        out_specs=(
            P("dp", None, "tensor"),
            P(None, "tensor", "dp", "section"),
            P(None, "tensor", "dp", "section"),
        ),
        check_vma=False,
    )
```
